32 devices in a mesh: pa: 1, row: 32 (over z, y, x, core).
Axes of the slice: x: 2, y: 2, z: 4, core: 2. Of those that a mesh axis runs over, the one named last changes fastest.
Arguments:
- raw_pulses: bfloat16 [64, 2, 16384], P(('pa', 'row')), may hold values from -6 to 6
- chirp_taps: bfloat16 [2, 512], replicated, may hold values from -0.1875 to 0.1875
- steer_angle: float32 [1, 64, 64], P('pa'), may hold values from -3.140625 to 3.140625
- interp_weights: bfloat16 [4, 1, 64, 128], P(None, 'pa', None, 'row'), may hold values from -3 to 3
- tile_phase: bfloat16 [1, 64, 128], P('pa', None, 'row'), may hold values from -3.140625 to 3.140625
- tap_offset: int32 [1, 64, 128], P('pa', None, 'row'), may hold values from -3 to 2
- image_slot: int32 [1, 64, 128], P('pa', None, 'row'), may hold values from 0 to 63
- tile_owner: int32 [1, 64, 128], P('pa', None, 'row'), may hold values from 0 to 31, as said below
Outputs:
- image: float32 [32, 64, 2, 128], P('row', 'pa')
The draws below stay inside these ranges and needn't reach their ends.
Inputs may be any that keep to these rules, and one draw needn't show every extreme that they name: `tile_owner`: among the tiles of one device (1 subapertures, all beams and 4 range tiles at one index of pa and of row) no owner is named more than 16 times; in every draw one owner, the same for all devices, is named exactly 16 times by the tiles of every device.
All inputs are finite; a program needn't handle non-finite values.
Results may differ from the reference program's by a relative error of at most 0.0085.
Values may be sent and summed in bfloat16 or wider, within the bound.
A program may use at most 64 MiB of HBM per device.

```python
import jax
import jax.numpy as jnp
from jax import lax

R = 16384
TAPS = 512
A = 64
BEAMS = 64
TILE = 128
IMG_ROWS = 64
OWNERS = 32
GROUPS = 1
P_SIZE = 64
NSUB = 1
NRT = 128
SUB_DEV = 1
RT_DEV = 4
TILES_DEV = 256
CAP = 16
FAN = 4


def draw_tile_owner(key, part):
    heavy_owner = jax.random.randint(jax.random.fold_in(key, 11), (), 0, OWNERS)
    block_keys = jax.random.split(jax.random.fold_in(key, 12), GROUPS * OWNERS)

    def one_block(block_key):
        key_one, key_two = jax.random.split(block_key)
        scattered = jax.random.permutation(key_one, (OWNERS - 1) * CAP)[:TILES_DEV - CAP] // CAP
        scattered = (scattered + (scattered >= heavy_owner).astype(jnp.int32)).astype(jnp.int32)
        listed = jnp.concatenate([jnp.full((CAP,), heavy_owner, jnp.int32), scattered])
        return listed[jax.random.permutation(key_two, TILES_DEV)]
    blocks = jax.vmap(one_block)(block_keys)
    blocks = blocks.reshape(GROUPS, OWNERS, SUB_DEV, BEAMS, RT_DEV)
    return blocks.transpose(0, 2, 3, 1, 4).reshape(NSUB, BEAMS, NRT).astype(jnp.int32)


def set_ends(entries, rng, low, top_value):
    index_at = [jax.random.randint(jax.random.fold_in(rng, axis), (), 0, length) for axis, length in enumerate(entries.shape)]
    main_axis = entries.shape.index(max(entries.shape))
    next_to = index_at[:main_axis] + [(index_at[main_axis] + 1) % entries.shape[main_axis]] + index_at[main_axis + 1:]
    return entries.at[tuple(index_at)].set(low).at[tuple(next_to)].set(top_value)


def steps_of(rng, shape, cuts, smallest, largest):
    loudness, own = 1.0, jax.random.fold_in(rng, 6)
    for dim, blocks in cuts:
        draws = jnp.exp(jax.random.uniform(jax.random.fold_in(own, dim), (blocks,), jnp.float32, smallest / len(cuts), largest / len(cuts)))
        loudness = loudness * jnp.repeat(draws, shape[dim] // blocks).reshape([-1 if axis == dim else 1 for axis in range(len(shape))])
    return loudness


def centred(rng, dims, width, most, pieces=(), held_as=jnp.bfloat16):
    level = steps_of(rng, dims, pieces, -0.22, 0.18) if pieces else 1.0
    values = jax.random.normal(rng, dims, jnp.float32) * width * level
    return jnp.minimum(jnp.maximum(values, -most), most).astype(held_as)


def setup_inputs(seed: int = 0) -> dict:
    keys = jax.random.split(jax.random.key(seed), 9)
    return {
        "raw_pulses": centred(keys[0], (P_SIZE, 2, R), 1.0, 6.0, ((0, 32),)),
        "chirp_taps": centred(keys[1], (2, TAPS), (2 * TAPS) ** -0.5, 0.1875),
        "steer_angle": jnp.clip(jax.random.uniform(keys[2], (NSUB, A, BEAMS), jnp.float32, -3.140625, 3.140625), -3.140625, 3.140625),
        "interp_weights": centred(keys[3], (4, NSUB, BEAMS, NRT), 0.5, 3.0, ((3, 32),)),
        "tile_phase": jnp.clip(jax.random.uniform(keys[4], (NSUB, BEAMS, NRT), jnp.float32, -3.140625, 3.140625), -3.140625, 3.140625).astype(jnp.bfloat16),
        "tap_offset": set_ends(jax.random.randint(keys[5], (NSUB, BEAMS, NRT), -3, 3), jax.random.fold_in(keys[5], 1), -3, 2).astype(jnp.int32),
        "image_slot": set_ends(jax.random.randint(keys[6], (NSUB, BEAMS, NRT), 0, IMG_ROWS), jax.random.fold_in(keys[6], 1), 0, IMG_ROWS - 1).astype(jnp.int32),
        "tile_owner": draw_tile_owner(jax.random.fold_in(keys[8], 71), 0),
    }


def band_of(taps):
    extended = jnp.concatenate([taps, jnp.zeros((TAPS + 1,), taps.dtype)])
    repeated = jnp.tile(extended, TAPS)[: 2 * TAPS * TAPS]
    return repeated.reshape(TAPS, 2 * TAPS).T


def toeplitz_matrix(chirp_taps):
    real_taps = band_of(chirp_taps[0])
    imag_taps = band_of(chirp_taps[1])
    upper = jnp.concatenate([real_taps, -imag_taps], 1)
    lower = jnp.concatenate([imag_taps, real_taps], 1)
    return jnp.concatenate([upper, lower], 0)


def compress(pulses, matrix):
    count_pulses = pulses.shape[0]
    length = pulses.shape[2]
    block_count = length // TAPS
    padded = jnp.pad(pulses, ((0, 0), (0, 0), (0, TAPS)))
    front_half = padded[:, :, :length].reshape(count_pulses, 2, block_count, TAPS)
    back_half = padded[:, :, TAPS:].reshape(count_pulses, 2, block_count, TAPS)
    extended = jnp.concatenate([front_half, back_half], 3)
    extended = extended.transpose(0, 2, 1, 3).reshape(count_pulses * block_count, 4 * TAPS)
    product = jnp.dot(extended, matrix, preferred_element_type=jnp.float32)
    product = product.reshape(count_pulses, block_count, 2, TAPS).transpose(0, 2, 1, 3)
    return product.reshape(count_pulses, 2, length).astype(jnp.bfloat16)


def beamform(grouped, angles):
    steering = jnp.concatenate([jnp.cos(angles), jnp.sin(angles)], 2).astype(jnp.bfloat16)
    steering = steering.astype(jnp.float32)
    from_real = jnp.einsum("sac,sar->scr", steering, grouped[:, :, 0].astype(jnp.float32))
    from_imag = jnp.einsum("sac,sar->scr", steering, grouped[:, :, 1].astype(jnp.float32))
    beam_count = angles.shape[2]
    beam_real = from_real[:, :beam_count] - from_imag[:, beam_count:]
    beam_imag = from_imag[:, :beam_count] + from_real[:, beam_count:]
    norm_factor = angles.shape[1] ** -0.5
    return (jnp.stack([beam_real, beam_imag], 2) * norm_factor).astype(jnp.bfloat16)


def interpolate(beam_tiles, weights, phases, offsets):
    padded = jnp.pad(beam_tiles.astype(jnp.float32), ((0, 0), (0, 0), (4, 4)))
    shift_values = jnp.arange(-4, 5, dtype=jnp.int32)
    tap_index = jnp.arange(4, dtype=jnp.int32)
    matches = (offsets[:, None, None] + tap_index[None, None, :] - 1) == shift_values[None, :, None]
    band_coeffs = jnp.sum(jnp.where(matches, weights.astype(jnp.float32)[:, None, :], 0.0), 2)
    summed_taps = band_coeffs[:, 0, None, None] * padded[:, :, 0:TILE]
    for position in range(1, 9):
        summed_taps = summed_taps + band_coeffs[:, position, None, None] * padded[:, :, position:position + TILE]
    cosine = jnp.cos(phases.astype(jnp.float32))[:, None]
    sine_part = jnp.sin(phases.astype(jnp.float32))[:, None]
    out_real = cosine * summed_taps[:, 0] - sine_part * summed_taps[:, 1]
    out_imag = sine_part * summed_taps[:, 0] + cosine * summed_taps[:, 1]
    return jnp.stack([out_real, out_imag], 1).astype(jnp.bfloat16)


def reference(raw_pulses, chirp_taps, steer_angle, interp_weights, tile_phase, tap_offset, image_slot, tile_owner):
    matrix = toeplitz_matrix(chirp_taps)

    def one_subaperture(image_sum, sub_index):
        pulses = lax.dynamic_slice_in_dim(raw_pulses, sub_index * A, A, 0)
        compressed = compress(pulses, matrix)
        formed = beamform(compressed[None], steer_angle[sub_index][None])[0]
        beam_tiles = formed.reshape(BEAMS, 2, NRT, TILE).transpose(0, 2, 1, 3).reshape(BEAMS * NRT, 2, TILE)
        weights = interp_weights[:, sub_index].reshape(4, BEAMS * NRT).T
        phases = tile_phase[sub_index].reshape(BEAMS * NRT)
        offsets = tap_offset[sub_index].reshape(BEAMS * NRT)
        targets = tile_owner[sub_index].reshape(BEAMS * NRT) * IMG_ROWS + image_slot[sub_index].reshape(BEAMS * NRT)
        shifted = interpolate(beam_tiles, weights, phases, offsets)
        flat_tiles = shifted.reshape(BEAMS * NRT, 2 * TILE).astype(jnp.float32)
        image_sum = image_sum + jax.ops.segment_sum(flat_tiles, targets, OWNERS * IMG_ROWS)
        return image_sum, None

    start_image = jnp.zeros((OWNERS * IMG_ROWS, 2 * TILE), jnp.float32)
    image_sum, unused_out = lax.scan(one_subaperture, start_image, jnp.arange(NSUB, dtype=jnp.int32))
    return (image_sum * (float(FAN) ** -0.5)).reshape(OWNERS, IMG_ROWS, 2, TILE)
```

```python
import functools

import jax
import jax.numpy as jnp
from jax import lax
from jax.experimental import pallas as pl
from jax.experimental.pallas import tpu as pltpu
from jax.sharding import PartitionSpec as P

LANES = 128
IMG_ROWS = 64
F32 = jnp.float32
BF16 = jnp.bfloat16
NT = (((1,), (1,)), ((), ()))
TN = (((0,), (0,)), ((), ()))
SHIFTS = tuple(range(-4, 5))


def iota(shape, dim):
    return lax.broadcasted_iota(jnp.int32, shape, dim)


def one_hot(cond):
    return jnp.where(cond, 1.0, 0.0)


def body(
    n,
    rows_out,
    x_ref,
    taps_ref,
    angle_ref,
    weight_ref,
    phase_ref,
    offset_ref,
    slot_ref,
    owner_ref,
    out_ref,
    xs,
    send_one,
    recv_one,
    send_slot,
    recv_slot,
    send_two,
    recv_two,
    steer,
    coeff,
    pack,
    sems,
):
    me = lax.axis_index("row")
    pulses, _, length = x_ref.shape
    blocks = length // LANES
    reach = taps_ref.shape[1] // LANES
    group = 2 * blocks // n
    width = pulses * group
    tiles = group // 2
    count_a, count_beams = angle_ref.shape
    count_tiles = tiles * count_beams
    capacity = send_two.shape[1]

    barrier = pltpu.get_barrier_semaphore()

    def greet(i, carry):
        pl.semaphore_signal(barrier, inc=1, device_id={"row": lax.rem(me + i, n)})
        return carry

    lax.fori_loop(1, n, greet, 0)

    for p in range(pulses):
        for b in range(blocks):
            piece = x_ref[p, :, b * LANES : (b + 1) * LANES]
            xs[p, 2 * b : 2 * b + 2, :] = piece.astype(F32)
        xs[p, 2 * blocks :, :] = jnp.zeros((2 * reach, LANES), F32)
    keep = iota((LANES, LANES), 1) >= iota((LANES, LANES), 0)
    zero = jnp.zeros((LANES, LANES), F32)
    halves = []
    for c in range(2):
        rolled = []
        for j in range(reach):
            row = taps_ref[c : c + 1, j * LANES : (j + 1) * LANES].astype(F32)
            row = jnp.broadcast_to(row, (LANES, LANES))
            rolled.append(pltpu.roll(row, 0, 1, stride=1, stride_axis=0))
        rolled = [zero] + rolled + [zero]
        halves.append(
            jnp.concatenate(
                [jnp.where(keep, rolled[j + 1], rolled[j]).astype(BF16) for j in range(reach + 1)], 1
            )
        )
    band = jnp.concatenate(halves, 0)
    outs = []
    parity = iota((2 * blocks, LANES), 0) % 2 == 0
    for p in range(pulses):
        window = jnp.concatenate(
            [xs[p, 2 * j : 2 * j + 2 * blocks, :].astype(BF16) for j in range(reach + 1)], 1
        )
        product = lax.dot_general(window, band, NT, preferred_element_type=F32)
        first, second = product[:, :LANES], product[:, LANES:]
        crossed = jnp.where(
            parity, pltpu.roll(second, 2 * blocks - 1, 0), -pltpu.roll(second, 1, 0)
        )
        outs.append((first + crossed).reshape(n, group, LANES))
    send_one[...] = jnp.concatenate(outs, 1).astype(BF16)

    pl.semaphore_wait(barrier, n - 1)

    def exchange(source, target, send_sem, recv_sem):
        def push(i, carry):
            to = lax.rem(me + i, n)
            pltpu.make_async_remote_copy(
                src_ref=source.at[to],
                dst_ref=target.at[me],
                send_sem=send_sem,
                recv_sem=recv_sem,
                device_id={"row": to},
            ).start()
            return carry

        lax.fori_loop(1, n, push, 0)
        pltpu.make_async_copy(source.at[me], target.at[me], recv_sem).start()

    def arrived(target, recv_sem):
        pltpu.make_async_copy(target, target, recv_sem).wait()

    def departed(source, send_sem):
        part = source.at[pl.ds(0, n - 1)]
        pltpu.make_async_copy(part, part, send_sem).wait()

    exchange(send_one, recv_one, sems.at[0], sems.at[1])

    owner = jnp.concatenate([owner_ref[:, t : t + 1] for t in range(tiles)], 0)
    slot = jnp.concatenate([slot_ref[:, t : t + 1] for t in range(tiles)], 0)
    member = one_hot(owner == iota((count_tiles, LANES), 1))
    before = one_hot(iota((count_tiles, count_tiles), 1) < iota((count_tiles, count_tiles), 0))
    ahead = jnp.dot(before.astype(BF16), member.astype(BF16), preferred_element_type=F32)
    rank = jnp.sum(ahead * member, 1, keepdims=True).astype(jnp.int32)
    ranked = jnp.where(rank == iota((count_tiles, LANES), 1), slot.astype(F32), 0.0)
    slots = lax.dot_general(
        member.astype(BF16), ranked.astype(BF16), TN, preferred_element_type=F32
    )
    send_slot[...] = slots[:n].reshape(n, 1, LANES)
    exchange(send_slot, recv_slot, sems.at[2], sems.at[3])
    place = owner * capacity + rank
    spread = one_hot(place == iota((count_tiles, n * capacity), 1))
    pack[...] = spread.T.astype(BF16)

    span = n * width
    pulse_of = iota((count_a, span), 1) // group == iota((count_a, span), 0)
    expand = one_hot(pulse_of).astype(BF16)
    angles = angle_ref[...]
    cosine = lax.dot_general(
        jnp.cos(angles).astype(BF16), expand, TN, preferred_element_type=F32
    )
    sine = lax.dot_general(
        jnp.sin(angles).astype(BF16), expand, TN, preferred_element_type=F32
    )
    column = iota((count_beams, span), 1) % group
    even = column % 2 == 0
    real_row = jnp.where(even, cosine, -sine)
    imag_row = jnp.where(even, sine, cosine)
    for t in range(tiles):
        here = column // 2 == t
        base = 2 * t * count_beams
        steer[base : base + count_beams, :] = jnp.where(here, real_row, 0.0).astype(BF16)
        base += count_beams
        steer[base : base + count_beams, :] = jnp.where(here, imag_row, 0.0).astype(BF16)

    lane = iota((count_beams, LANES), 1)
    offsets = offset_ref[...]
    weights = weight_ref[...].astype(F32)
    for s, shift in enumerate(SHIFTS):
        level = jnp.zeros((count_beams, tiles), F32)
        for k in range(4):
            level = level + jnp.where(offsets + (k - 1) == shift, weights[k], 0.0)
        inside = (lane + shift >= 0) & (lane + shift < LANES)
        for t in range(tiles):
            coeff[t, s] = jnp.where(inside, level[:, t : t + 1], 0.0)
    phases = phase_ref[...].astype(F32)
    cos_phase, sin_phase = jnp.cos(phases), jnp.sin(phases)

    arrived(recv_one, sems.at[1])
    turned = recv_one[...].reshape(span, LANES)
    formed = jnp.dot(steer[...], turned, preferred_element_type=F32)
    formed = (formed * count_a ** (-0.5)).astype(BF16).astype(F32)
    shifted = []
    for t in range(tiles):
        summed = []
        for c in range(2):
            base = (2 * t + c) * count_beams
            x = formed[base : base + count_beams]
            total = coeff[t, 4] * x
            for s, shift in enumerate(SHIFTS):
                if shift != 0:
                    total = total + coeff[t, s] * pltpu.roll(x, (-shift) % LANES, 1)
            summed.append(total)
        cos_here, sin_here = cos_phase[:, t : t + 1], sin_phase[:, t : t + 1]
        real = cos_here * summed[0] - sin_here * summed[1]
        imag = sin_here * summed[0] + cos_here * summed[1]
        shifted.append(jnp.concatenate([real, imag], 1).astype(BF16))
    ready = jnp.dot(pack[...], jnp.concatenate(shifted, 0), preferred_element_type=F32)
    send_two[...] = ready.astype(BF16).reshape(n, capacity, 2 * LANES)
    exchange(send_two, recv_two, sems.at[4], sems.at[5])

    arrived(recv_slot, sems.at[3])
    total_slots = n * capacity
    got = recv_slot[...].reshape(n, LANES).astype(BF16)
    source_of = iota((total_slots, n), 0) // capacity == iota((total_slots, n), 1)
    got = jnp.dot(one_hot(source_of).astype(BF16), got, preferred_element_type=F32)
    wanted = iota((total_slots, LANES), 0) % capacity == iota((total_slots, LANES), 1)
    got = jnp.sum(jnp.where(wanted, got, 0.0), 1, keepdims=True).astype(jnp.int32)
    select = one_hot(got == iota((total_slots, LANES), 1)).T[:rows_out].astype(BF16)
    arrived(recv_two, sems.at[5])
    landed = recv_two[...].reshape(total_slots, 2 * LANES)
    out_ref[...] = jnp.dot(select, landed, preferred_element_type=F32)
    departed(send_one, sems.at[0])
    departed(send_slot, sems.at[2])
    departed(send_two, sems.at[4])


def per_device(
    n,
    pa,
    raw_pulses,
    chirp_taps,
    steer_angle,
    interp_weights,
    tile_phase,
    tap_offset,
    image_slot,
    tile_owner,
):
    pulses, _, length = raw_pulses.shape
    _, count_a, count_beams = steer_angle.shape
    tiles = tile_owner.shape[2]
    count_tiles = count_beams * tiles
    capacity = 2 * count_tiles // n
    blocks = length // LANES
    width = pulses * 2 * blocks // n
    reach = chirp_taps.shape[1] // LANES
    image_part = pl.pallas_call(
        functools.partial(body, n, IMG_ROWS),
        out_shape=jax.ShapeDtypeStruct((IMG_ROWS, 2 * LANES), F32),
        in_specs=[pl.BlockSpec(memory_space=pltpu.VMEM)] * 8,
        out_specs=pl.BlockSpec(memory_space=pltpu.VMEM),
        scratch_shapes=[
            pltpu.VMEM((pulses, 2 * blocks + 2 * reach, LANES), F32),
            pltpu.VMEM((n, width, LANES), BF16),
            pltpu.VMEM((n, width, LANES), BF16),
            pltpu.VMEM((n, 1, LANES), F32),
            pltpu.VMEM((n, 1, LANES), F32),
            pltpu.VMEM((n, capacity, 2 * LANES), BF16),
            pltpu.VMEM((n, capacity, 2 * LANES), BF16),
            pltpu.VMEM((2 * tiles * count_beams, n * width), BF16),
            pltpu.VMEM((tiles, len(SHIFTS), count_beams, LANES), F32),
            pltpu.VMEM((n * capacity, count_tiles), BF16),
            pltpu.SemaphoreType.DMA((6,)),
        ],
        compiler_params=pltpu.CompilerParams(
            collective_id=0, has_side_effects=True, vmem_limit_bytes=48 << 20
        ),
    )(
        raw_pulses,
        chirp_taps,
        steer_angle.reshape(count_a, count_beams),
        interp_weights.reshape(4, count_beams, tiles),
        tile_phase.reshape(count_beams, tiles),
        tap_offset.reshape(count_beams, tiles),
        image_slot.reshape(count_beams, tiles),
        tile_owner.reshape(count_beams, tiles),
    )
    image_part = image_part.reshape(IMG_ROWS, 2, LANES)
    if pa > 1:
        image_part = lax.psum_scatter(image_part, "pa", scatter_dimension=0, tiled=True)
    spread_factor = float(pa * count_tiles // IMG_ROWS) ** (-0.5)
    return (image_part * spread_factor)[None]


def solution(mesh):
    placed = (
        P(("pa", "row"), None, None),
        P(),
        P("pa", None, None),
        P(None, "pa", None, "row"),
        P("pa", None, "row"),
        P("pa", None, "row"),
        P("pa", None, "row"),
        P("pa", None, "row"),
    )
    return jax.shard_map(
        functools.partial(per_device, mesh.shape["row"], mesh.shape["pa"]),
        mesh=mesh,
        in_specs=placed,
        out_specs=P("row", "pa", None, None),
        check_vma=False,
    )
```

```python
import functools

import jax
import jax.numpy as jnp
from jax import lax
from jax.experimental import pallas as pl
from jax.experimental.pallas import tpu as pltpu
from jax.sharding import PartitionSpec as P

LANES = 128
IMG_ROWS = 64
F32 = jnp.float32
BF16 = jnp.bfloat16
NT = (((1,), (1,)), ((), ()))
TN = (((0,), (0,)), ((), ()))
SHIFTS = tuple(range(-4, 5))


def iota(shape, dim):
    return lax.broadcasted_iota(jnp.int32, shape, dim)


def one_hot(cond):
    return jnp.where(cond, 1.0, 0.0)


def body(
    n,
    rows_out,
    scale,
    x_hbm,
    taps_hbm,
    angle_hbm,
    owner_hbm,
    slot_hbm,
    weight_hbm,
    phase_hbm,
    offset_hbm,
    out_ref,
    x_ref,
    taps_ref,
    angle_ref,
    owner_ref,
    slot_ref,
    weight_ref,
    phase_ref,
    offset_ref,
    xs,
    send_one,
    recv_one,
    send_slot,
    recv_slot,
    send_two,
    recv_two,
    steer,
    coeff,
    pack,
    sems,
    load_sems,
):
    me = lax.axis_index("row")
    pulses, _, length = x_ref.shape
    blocks = length // LANES
    reach = taps_ref.shape[1] // LANES
    group = 2 * blocks // n
    width = pulses * group
    tiles = group // 2
    count_a, count_beams = angle_ref.shape
    count_tiles = tiles * count_beams
    capacity = send_two.shape[1]

    given = (x_hbm, taps_hbm, angle_hbm, owner_hbm, slot_hbm, weight_hbm, phase_hbm, offset_hbm)
    held = (x_ref, taps_ref, angle_ref, owner_ref, slot_ref, weight_ref, phase_ref, offset_ref)
    held_copies = [
        pltpu.make_async_copy(source, target, load_sems.at[index])
        for index, (source, target) in enumerate(zip(given, held))
    ]
    for copy in held_copies:
        copy.start()
    barrier = pltpu.get_barrier_semaphore()

    def greet(i, carry):
        pl.semaphore_signal(barrier, inc=1, device_id={"row": lax.rem(me + i, n)})
        return carry

    lax.fori_loop(1, n, greet, 0)

    held_copies[0].wait()
    for p in range(pulses):
        for b in range(blocks):
            piece = x_ref[p, :, b * LANES : (b + 1) * LANES]
            xs[p, 2 * b : 2 * b + 2, :] = piece.astype(F32)
        xs[p, 2 * blocks :, :] = jnp.zeros((2 * reach, LANES), F32)
    keep = iota((LANES, LANES), 1) >= iota((LANES, LANES), 0)
    zero = jnp.zeros((LANES, LANES), F32)
    held_copies[1].wait()
    halves = []
    for c in range(2):
        rolled = []
        for j in range(reach):
            row = taps_ref[c : c + 1, j * LANES : (j + 1) * LANES].astype(F32)
            row = jnp.broadcast_to(row, (LANES, LANES))
            rolled.append(pltpu.roll(row, 0, 1, stride=1, stride_axis=0))
        rolled = [zero] + rolled + [zero]
        halves.append(
            jnp.concatenate(
                [jnp.where(keep, rolled[j + 1], rolled[j]).astype(BF16) for j in range(reach + 1)], 1
            )
        )
    band = jnp.concatenate(halves, 0)
    outs = []
    parity = iota((2 * blocks, LANES), 0) % 2 == 0
    for p in range(pulses):
        window = jnp.concatenate(
            [xs[p, 2 * j : 2 * j + 2 * blocks, :].astype(BF16) for j in range(reach + 1)], 1
        )
        product = lax.dot_general(window, band, NT, preferred_element_type=F32)
        first, second = product[:, :LANES], product[:, LANES:]
        crossed = jnp.where(
            parity, pltpu.roll(second, 2 * blocks - 1, 0), -pltpu.roll(second, 1, 0)
        )
        outs.append((first + crossed).reshape(n, group, LANES))
    send_one[...] = jnp.concatenate(outs, 1).astype(BF16)

    pl.semaphore_wait(barrier, n - 1)

    def exchange(source, target, send_sem, recv_sem):
        def push(i, carry):
            to = lax.rem(me + i, n)
            pltpu.make_async_remote_copy(
                src_ref=source.at[to],
                dst_ref=target.at[me],
                send_sem=send_sem,
                recv_sem=recv_sem,
                device_id={"row": to},
            ).start()
            return carry

        lax.fori_loop(1, n, push, 0)
        pltpu.make_async_copy(source.at[me], target.at[me], recv_sem).start()

    def arrived(target, recv_sem):
        pltpu.make_async_copy(target, target, recv_sem).wait()

    def departed(source, send_sem):
        part = source.at[pl.ds(0, n - 1)]
        pltpu.make_async_copy(part, part, send_sem).wait()

    exchange(send_one, recv_one, sems.at[0], sems.at[1])

    held_copies[3].wait()
    held_copies[4].wait()
    owner = jnp.concatenate([owner_ref[t : t + 1, :] for t in range(tiles)], 1)
    slot = jnp.concatenate([slot_ref[t : t + 1, :] for t in range(tiles)], 1)
    member = one_hot(owner == iota((n, count_tiles), 0))
    before = one_hot(iota((count_tiles, count_tiles), 0) < iota((count_tiles, count_tiles), 1))
    ahead = jnp.dot(member.astype(BF16), before.astype(BF16), preferred_element_type=F32)
    rank = jnp.sum(ahead * member, 0, keepdims=True).astype(jnp.int32)
    ranked = jnp.where(rank == iota((LANES, count_tiles), 0), slot.astype(F32), 0.0)
    slots = lax.dot_general(
        member.astype(BF16), ranked.astype(BF16), NT, preferred_element_type=F32
    )
    send_slot[...] = slots.reshape(n, 1, LANES)
    exchange(send_slot, recv_slot, sems.at[2], sems.at[3])
    place = owner * capacity + rank
    pack[...] = one_hot(place == iota((n * capacity, count_tiles), 0)).astype(BF16)

    held_copies[2].wait()
    span = n * width
    pulse_of = iota((count_a, span), 1) // group == iota((count_a, span), 0)
    expand = one_hot(pulse_of).astype(BF16)
    angles = angle_ref[...]
    cosine = lax.dot_general(
        jnp.cos(angles).astype(BF16), expand, TN, preferred_element_type=F32
    )
    sine = lax.dot_general(
        jnp.sin(angles).astype(BF16), expand, TN, preferred_element_type=F32
    )
    column = iota((count_beams, span), 1) % group
    even = column % 2 == 0
    real_row = jnp.where(even, cosine, -sine)
    imag_row = jnp.where(even, sine, cosine)
    for t in range(tiles):
        here = column // 2 == t
        base = 2 * t * count_beams
        steer[base : base + count_beams, :] = jnp.where(here, real_row, 0.0).astype(BF16)
        base += count_beams
        steer[base : base + count_beams, :] = jnp.where(here, imag_row, 0.0).astype(BF16)

    for index in (5, 6, 7):
        held_copies[index].wait()
    lane = iota((count_beams, LANES), 1)
    offsets = offset_ref[...]
    weights = weight_ref[...].astype(F32)
    levels = []
    for shift in SHIFTS:
        level = jnp.zeros((tiles, count_beams), F32)
        for k in range(4):
            level = level + jnp.where(offsets + (k - 1) == shift, weights[k], 0.0)
        levels.append(level)
    phases = phase_ref[...].astype(F32)
    levels += [jnp.cos(phases), jnp.sin(phases)]
    spare = LANES - len(levels) * tiles
    levels = jnp.concatenate(levels + [jnp.zeros((spare, count_beams), F32)], 0).T
    for s, shift in enumerate(SHIFTS):
        inside = (lane + shift >= 0) & (lane + shift < LANES)
        for t in range(tiles):
            at = s * tiles + t
            coeff[t, s] = jnp.where(inside, levels[:, at : at + 1], 0.0)
    for s in range(len(SHIFTS), len(SHIFTS) + 2):
        for t in range(tiles):
            at = s * tiles + t
            coeff[t, s] = jnp.broadcast_to(levels[:, at : at + 1], (count_beams, LANES))

    arrived(recv_one, sems.at[1])
    turned = recv_one[...].reshape(span, LANES)
    formed = jnp.dot(steer[...], turned, preferred_element_type=F32)
    formed = (formed * count_a ** (-0.5)).astype(BF16).astype(F32)
    shifted = []
    for t in range(tiles):
        summed = []
        for c in range(2):
            base = (2 * t + c) * count_beams
            x = formed[base : base + count_beams]
            total = coeff[t, 4] * x
            for s, shift in enumerate(SHIFTS):
                if shift != 0:
                    total = total + coeff[t, s] * pltpu.roll(x, (-shift) % LANES, 1)
            summed.append(total)
        cos_here, sin_here = coeff[t, len(SHIFTS)], coeff[t, len(SHIFTS) + 1]
        real = cos_here * summed[0] - sin_here * summed[1]
        imag = sin_here * summed[0] + cos_here * summed[1]
        shifted.append(jnp.concatenate([real, imag], 1).astype(BF16))
    ready = jnp.dot(pack[...], jnp.concatenate(shifted, 0), preferred_element_type=F32)
    send_two[...] = ready.astype(BF16).reshape(n, capacity, 2 * LANES)
    exchange(send_two, recv_two, sems.at[4], sems.at[5])

    arrived(recv_slot, sems.at[3])
    total_slots = n * capacity
    got = recv_slot[...].reshape(n, LANES).astype(BF16)
    source_of = iota((total_slots, n), 0) // capacity == iota((total_slots, n), 1)
    got = jnp.dot(one_hot(source_of).astype(BF16), got, preferred_element_type=F32)
    wanted = iota((total_slots, LANES), 0) % capacity == iota((total_slots, LANES), 1)
    got = jnp.sum(jnp.where(wanted, got, 0.0), 1, keepdims=True).astype(jnp.int32)
    select = one_hot(got == iota((total_slots, LANES), 1)).T[:rows_out].astype(BF16)
    arrived(recv_two, sems.at[5])
    landed = recv_two[...].reshape(total_slots, 2 * LANES)
    image = jnp.dot(select, landed, preferred_element_type=F32) * scale
    out_ref[:, 0, :] = image[:, :LANES]
    out_ref[:, 1, :] = image[:, LANES:]
    departed(send_one, sems.at[0])
    departed(send_slot, sems.at[2])
    departed(send_two, sems.at[4])


def per_device(
    n,
    pa,
    raw_pulses,
    chirp_taps,
    steer_angle,
    interp_weights,
    tile_phase,
    tap_offset,
    image_slot,
    tile_owner,
):
    pulses, _, length = raw_pulses.shape
    _, count_a, count_beams = steer_angle.shape
    tiles = tile_owner.shape[2]
    count_tiles = count_beams * tiles
    capacity = 2 * count_tiles // n
    blocks = length // LANES
    width = pulses * 2 * blocks // n
    reach = chirp_taps.shape[1] // LANES
    spread_factor = float(pa * count_tiles // IMG_ROWS) ** (-0.5)
    operands = (
        raw_pulses,
        chirp_taps,
        steer_angle.reshape(count_a, count_beams),
        tile_owner.transpose(0, 2, 1).reshape(tiles, count_beams),
        image_slot.transpose(0, 2, 1).reshape(tiles, count_beams),
        interp_weights.transpose(0, 1, 3, 2).reshape(4, tiles, count_beams),
        tile_phase.transpose(0, 2, 1).reshape(tiles, count_beams),
        tap_offset.transpose(0, 2, 1).reshape(tiles, count_beams),
    )
    image_part = pl.pallas_call(
        functools.partial(body, n, IMG_ROWS, spread_factor),
        out_shape=jax.ShapeDtypeStruct((IMG_ROWS, 2, LANES), F32),
        in_specs=[pl.BlockSpec(memory_space=pltpu.HBM)] * len(operands),
        out_specs=pl.BlockSpec(memory_space=pltpu.VMEM),
        scratch_shapes=[pltpu.VMEM(x.shape, x.dtype) for x in operands]
        + [
            pltpu.VMEM((pulses, 2 * blocks + 2 * reach, LANES), F32),
            pltpu.VMEM((n, width, LANES), BF16),
            pltpu.VMEM((n, width, LANES), BF16),
            pltpu.VMEM((n, 1, LANES), F32),
            pltpu.VMEM((n, 1, LANES), F32),
            pltpu.VMEM((n, capacity, 2 * LANES), BF16),
            pltpu.VMEM((n, capacity, 2 * LANES), BF16),
            pltpu.VMEM((2 * tiles * count_beams, n * width), BF16),
            pltpu.VMEM((tiles, len(SHIFTS) + 2, count_beams, LANES), F32),
            pltpu.VMEM((n * capacity, count_tiles), BF16),
            pltpu.SemaphoreType.DMA((6,)),
            pltpu.SemaphoreType.DMA((len(operands),)),
        ],
        compiler_params=pltpu.CompilerParams(
            collective_id=0, has_side_effects=True, vmem_limit_bytes=62 << 20
        ),
    )(*operands)
    if pa > 1:
        image_part = lax.psum_scatter(image_part, "pa", scatter_dimension=0, tiled=True)
    return image_part[None]


def solution(mesh):
    placed = (
        P(("pa", "row"), None, None),
        P(),
        P("pa", None, None),
        P(None, "pa", None, "row"),
        P("pa", None, "row"),
        P("pa", None, "row"),
        P("pa", None, "row"),
        P("pa", None, "row"),
    )
    return jax.shard_map(
        functools.partial(per_device, mesh.shape["row"], mesh.shape["pa"]),
        mesh=mesh,
        in_specs=placed,
        out_specs=P("row", "pa", None, None),
        check_vma=False,
    )
```

```python
import functools

import jax
import jax.numpy as jnp
from jax import lax
from jax.experimental import pallas as pl
from jax.experimental.pallas import tpu as pltpu
from jax.sharding import PartitionSpec as P

LANES = 128
IMG_ROWS = 64
F32 = jnp.float32
BF16 = jnp.bfloat16
NT = (((1,), (1,)), ((), ()))
TN = (((0,), (0,)), ((), ()))
SHIFTS = tuple(range(-4, 5))


def iota(shape, dim):
    return lax.broadcasted_iota(jnp.int32, shape, dim)


def one_hot(cond):
    return jnp.where(cond, 1.0, 0.0)


def body(
    n,
    rows_out,
    scale,
    x_hbm,
    taps_hbm,
    angle_hbm,
    owner_hbm,
    slot_hbm,
    weight_hbm,
    phase_hbm,
    offset_hbm,
    out_ref,
    x_ref,
    taps_ref,
    angle_ref,
    owner_ref,
    slot_ref,
    weight_ref,
    phase_ref,
    offset_ref,
    xs,
    send_one,
    recv_one,
    send_slot,
    recv_slot,
    send_two,
    recv_two,
    steer,
    coeff,
    pack,
    sems,
    load_sems,
):
    me = lax.axis_index("row")
    pulses, _, length = x_ref.shape
    blocks = length // LANES
    reach = taps_ref.shape[1] // LANES
    group = 2 * blocks // n
    width = pulses * group
    tiles = group // 2
    count_a, count_beams = angle_ref.shape
    count_tiles = tiles * count_beams
    capacity = send_two.shape[1]

    given = (x_hbm, taps_hbm, angle_hbm, owner_hbm, slot_hbm, weight_hbm, phase_hbm, offset_hbm)
    held = (x_ref, taps_ref, angle_ref, owner_ref, slot_ref, weight_ref, phase_ref, offset_ref)
    held_copies = [
        pltpu.make_async_copy(source, target, load_sems.at[index])
        for index, (source, target) in enumerate(zip(given, held))
    ]
    for copy in held_copies:
        copy.start()
    barrier = pltpu.get_barrier_semaphore()

    def greet(i, carry):
        pl.semaphore_signal(barrier, inc=1, device_id={"row": lax.rem(me + i, n)})
        return carry

    lax.fori_loop(1, n, greet, 0)

    held_copies[0].wait()
    for p in range(pulses):
        for b in range(blocks):
            piece = x_ref[p, :, b * LANES : (b + 1) * LANES]
            xs[p, 2 * b : 2 * b + 2, :] = piece.astype(F32)
        xs[p, 2 * blocks :, :] = jnp.zeros((2 * reach, LANES), F32)
    keep = iota((LANES, LANES), 1) >= iota((LANES, LANES), 0)
    zero = jnp.zeros((LANES, LANES), F32)
    held_copies[1].wait()
    halves = []
    for c in range(2):
        rolled = []
        for j in range(reach):
            row = taps_ref[c : c + 1, j * LANES : (j + 1) * LANES].astype(F32)
            row = jnp.broadcast_to(row, (LANES, LANES))
            rolled.append(pltpu.roll(row, 0, 1, stride=1, stride_axis=0))
        rolled = [zero] + rolled + [zero]
        halves.append(
            jnp.concatenate(
                [jnp.where(keep, rolled[j + 1], rolled[j]).astype(BF16) for j in range(reach + 1)], 1
            )
        )
    band = jnp.concatenate(halves, 0)
    outs = []
    parity = iota((2 * blocks, LANES), 0) % 2 == 0
    for p in range(pulses):
        window = jnp.concatenate(
            [xs[p, 2 * j : 2 * j + 2 * blocks, :].astype(BF16) for j in range(reach + 1)], 1
        )
        product = lax.dot_general(window, band, NT, preferred_element_type=F32)
        first, second = product[:, :LANES], product[:, LANES:]
        crossed = jnp.where(
            parity, pltpu.roll(second, 2 * blocks - 1, 0), -pltpu.roll(second, 1, 0)
        )
        outs.append((first + crossed).reshape(n, group, LANES))
    send_one[...] = jnp.concatenate(outs, 1).astype(BF16)

    pl.semaphore_wait(barrier, n - 1)

    def exchange(source, target, send_sem, recv_sem):
        def push(i, carry):
            to = lax.rem(me + i, n)
            pltpu.make_async_remote_copy(
                src_ref=source.at[to],
                dst_ref=target.at[me],
                send_sem=send_sem,
                recv_sem=recv_sem,
                device_id={"row": to},
            ).start()
            return carry

        lax.fori_loop(1, n, push, 0)
        pltpu.make_async_copy(source.at[me], target.at[me], recv_sem).start()

    def arrived(target, recv_sem):
        pltpu.make_async_copy(target, target, recv_sem).wait()

    def departed(source, send_sem):
        part = source.at[pl.ds(0, n - 1)]
        pltpu.make_async_copy(part, part, send_sem).wait()

    exchange(send_one, recv_one, sems.at[0], sems.at[1])

    held_copies[3].wait()
    held_copies[4].wait()
    owner = jnp.concatenate([owner_ref[t : t + 1, :] for t in range(tiles)], 1)
    slot = jnp.concatenate([slot_ref[t : t + 1, :] for t in range(tiles)], 1)
    member = one_hot(owner == iota((n, count_tiles), 0))
    before = one_hot(iota((count_tiles, count_tiles), 0) < iota((count_tiles, count_tiles), 1))
    ahead = jnp.dot(member.astype(BF16), before.astype(BF16), preferred_element_type=F32)
    rank = jnp.sum(ahead * member, 0, keepdims=True).astype(jnp.int32)
    ranked = jnp.where(rank == iota((LANES, count_tiles), 0), slot.astype(F32), 0.0)
    slots = lax.dot_general(
        member.astype(BF16), ranked.astype(BF16), NT, preferred_element_type=F32
    )
    send_slot[...] = slots.reshape(n, 1, LANES)
    exchange(send_slot, recv_slot, sems.at[2], sems.at[3])
    place = owner * capacity + rank
    pack[...] = one_hot(place == iota((n * capacity, count_tiles), 0)).astype(BF16)

    held_copies[2].wait()
    span = n * width
    pulse_of = iota((count_a, span), 1) // group == iota((count_a, span), 0)
    expand = one_hot(pulse_of).astype(BF16)
    angles = angle_ref[...]
    cosine = lax.dot_general(
        jnp.cos(angles).astype(BF16), expand, TN, preferred_element_type=F32
    )
    sine = lax.dot_general(
        jnp.sin(angles).astype(BF16), expand, TN, preferred_element_type=F32
    )
    column = iota((count_beams, span), 1) % group
    even = column % 2 == 0
    real_row = jnp.where(even, cosine, -sine)
    imag_row = jnp.where(even, sine, cosine)
    for t in range(tiles):
        here = column // 2 == t
        base = 2 * t * count_beams
        steer[base : base + count_beams, :] = jnp.where(here, real_row, 0.0).astype(BF16)
        base += count_beams
        steer[base : base + count_beams, :] = jnp.where(here, imag_row, 0.0).astype(BF16)

    for index in (5, 6, 7):
        held_copies[index].wait()
    lane = iota((count_beams, LANES), 1)
    offsets = offset_ref[...]
    weights = weight_ref[...].astype(F32)
    levels = []
    for shift in SHIFTS:
        level = jnp.zeros((tiles, count_beams), F32)
        for k in range(4):
            level = level + jnp.where(offsets + (k - 1) == shift, weights[k], 0.0)
        levels.append(level)
    phases = phase_ref[...].astype(F32)
    levels += [jnp.cos(phases), jnp.sin(phases)]
    spare = LANES - len(levels) * tiles
    levels = jnp.concatenate(levels + [jnp.zeros((spare, count_beams), F32)], 0).T
    for s, shift in enumerate(SHIFTS):
        inside = (lane + shift >= 0) & (lane + shift < LANES)
        for t in range(tiles):
            at = s * tiles + t
            coeff[t, s] = jnp.where(inside, levels[:, at : at + 1], 0.0)
    for s in range(len(SHIFTS), len(SHIFTS) + 2):
        for t in range(tiles):
            at = s * tiles + t
            coeff[t, s] = jnp.broadcast_to(levels[:, at : at + 1], (count_beams, LANES))

    arrived(recv_one, sems.at[1])
    turned = recv_one[...].reshape(span, LANES)
    formed = jnp.dot(steer[...], turned, preferred_element_type=F32)
    formed = (formed * count_a ** (-0.5)).astype(BF16).astype(F32)
    shifted = []
    for t in range(tiles):
        summed = []
        for c in range(2):
            base = (2 * t + c) * count_beams
            x = formed[base : base + count_beams]
            total = coeff[t, 4] * x
            for s, shift in enumerate(SHIFTS):
                if shift != 0:
                    total = total + coeff[t, s] * pltpu.roll(x, (-shift) % LANES, 1)
            summed.append(total)
        cos_here, sin_here = coeff[t, len(SHIFTS)], coeff[t, len(SHIFTS) + 1]
        real = cos_here * summed[0] - sin_here * summed[1]
        imag = sin_here * summed[0] + cos_here * summed[1]
        shifted.append(jnp.concatenate([real, imag], 1).astype(BF16))
    ready = jnp.dot(pack[...], jnp.concatenate(shifted, 0), preferred_element_type=F32)
    send_two[...] = ready.astype(BF16).reshape(n, capacity, 2 * LANES)
    exchange(send_two, recv_two, sems.at[4], sems.at[5])

    arrived(recv_slot, sems.at[3])
    total_slots = n * capacity
    got = recv_slot[...].reshape(n, LANES).astype(BF16)
    source_of = iota((total_slots, n), 0) // capacity == iota((total_slots, n), 1)
    got = jnp.dot(one_hot(source_of).astype(BF16), got, preferred_element_type=F32)
    wanted = iota((total_slots, LANES), 0) % capacity == iota((total_slots, LANES), 1)
    got = jnp.sum(jnp.where(wanted, got, 0.0), 1, keepdims=True).astype(jnp.int32)
    select = one_hot(got == iota((total_slots, LANES), 1)).T[:rows_out].astype(BF16)
    arrived(recv_two, sems.at[5])
    landed = recv_two[...].reshape(total_slots, 2 * LANES)
    image = jnp.dot(select, landed, preferred_element_type=F32) * scale
    out_ref[:, 0, :] = image[:, :LANES]
    out_ref[:, 1, :] = image[:, LANES:]
    departed(send_one, sems.at[0])
    departed(send_slot, sems.at[2])
    departed(send_two, sems.at[4])


def per_device(
    n,
    pa,
    raw_pulses,
    chirp_taps,
    steer_angle,
    interp_weights,
    tile_phase,
    tap_offset,
    image_slot,
    tile_owner,
):
    pulses, _, length = raw_pulses.shape
    _, count_a, count_beams = steer_angle.shape
    tiles = tile_owner.shape[2]
    count_tiles = count_beams * tiles
    capacity = 2 * count_tiles // n
    blocks = length // LANES
    width = pulses * 2 * blocks // n
    reach = chirp_taps.shape[1] // LANES
    spread_factor = float(pa * count_tiles // IMG_ROWS) ** (-0.5)
    operands = (
        raw_pulses,
        chirp_taps,
        steer_angle.reshape(count_a, count_beams),
        tile_owner.transpose(0, 2, 1).reshape(tiles, count_beams),
        image_slot.transpose(0, 2, 1).reshape(tiles, count_beams),
        interp_weights.transpose(0, 1, 3, 2).reshape(4, tiles, count_beams),
        tile_phase.transpose(0, 2, 1).reshape(tiles, count_beams),
        tap_offset.transpose(0, 2, 1).reshape(tiles, count_beams),
    )
    image_part = pl.pallas_call(
        functools.partial(body, n, IMG_ROWS, spread_factor),
        out_shape=pltpu.VMEM((IMG_ROWS, 2, LANES), F32),
        in_specs=[pl.BlockSpec(memory_space=pltpu.HBM)] * len(operands),
        out_specs=pl.BlockSpec(memory_space=pltpu.VMEM),
        scratch_shapes=[pltpu.VMEM(x.shape, x.dtype) for x in operands]
        + [
            pltpu.VMEM((pulses, 2 * blocks + 2 * reach, LANES), F32),
            pltpu.VMEM((n, width, LANES), BF16),
            pltpu.VMEM((n, width, LANES), BF16),
            pltpu.VMEM((n, 1, LANES), F32),
            pltpu.VMEM((n, 1, LANES), F32),
            pltpu.VMEM((n, capacity, 2 * LANES), BF16),
            pltpu.VMEM((n, capacity, 2 * LANES), BF16),
            pltpu.VMEM((2 * tiles * count_beams, n * width), BF16),
            pltpu.VMEM((tiles, len(SHIFTS) + 2, count_beams, LANES), F32),
            pltpu.VMEM((n * capacity, count_tiles), BF16),
            pltpu.SemaphoreType.DMA((6,)),
            pltpu.SemaphoreType.DMA((len(operands),)),
        ],
        compiler_params=pltpu.CompilerParams(
            collective_id=0, has_side_effects=True, vmem_limit_bytes=62 << 20
        ),
    )(*operands)
    if pa > 1:
        image_part = lax.psum_scatter(image_part, "pa", scatter_dimension=0, tiled=True)
    return image_part[None]


def solution(mesh):
    placed = (
        P(("pa", "row"), None, None),
        P(),
        P("pa", None, None),
        P(None, "pa", None, "row"),
        P("pa", None, "row"),
        P("pa", None, "row"),
        P("pa", None, "row"),
        P("pa", None, "row"),
    )
    return jax.shard_map(
        functools.partial(per_device, mesh.shape["row"], mesh.shape["pa"]),
        mesh=mesh,
        in_specs=placed,
        out_specs=P("row", "pa", None, None),
        check_vma=False,
    )
```
